32 devices in a mesh: seq: 8 (over y, x, core), tensor: 4 (over z).
Axes of the slice: x: 2, y: 2, z: 4, core: 2. Of those that a mesh axis runs over, the one named last changes fastest.
Arguments:
- tokens: bfloat16 [1024, 16384], P('seq', 'tensor'), may hold values from -100 to 100
- norm_gain: float32 [16384], P('tensor'), may hold values from 0.5 to 1.5
- projection_weight: bfloat16 [2048, 16384], P('tensor', 'seq'), may hold values from -1.5 to 1.5
- panel_index: int32 [1], replicated, may hold values from 0 to 31
Outputs:
- gram: float32 [16384, 16384], P('seq', 'tensor')
- factor_panel: bfloat16 [16384, 512], P('seq')
- projected: float32 [2048, 512], P('tensor', 'seq')
The draws below stay inside these ranges and needn't reach their ends.
All inputs are finite; a program needn't handle non-finite values.
Results may differ from the reference program's by a relative error of at most 0.0057.
Values may be sent and summed in bfloat16 or wider, within the bound.
No kernel may reach another device: no remote copies, remote signals or barrier semaphores. Data moves between devices by JAX's collectives and lax.ppermute only.
A program may use at most 128 MiB of HBM per device.

```python
import math
import jax
import jax.numpy as jnp
from jax import lax

D = 16384
PANEL = 512
TOKENS = 1024
KV_ROWS = 2048
NPANELS = 32


def draw_tokens(key, part):
    first, second = jax.random.split(key, 2)
    position = jnp.arange(D, dtype=jnp.float32) / D
    token_place = jnp.arange(TOKENS, dtype=jnp.float32)[:, None] / TOKENS
    values = jax.random.normal(first, (TOKENS, D), jnp.float32)
    row_scale = jnp.exp(math.log(10.0) * (-3.0 + 2.0 * token_place))
    values = values * row_scale
    rising = jnp.exp(0.5 * math.log(3.0) * position)
    rough = jax.random.uniform(second, (1, D), jnp.float32, 0.5, 1.5)
    result = jnp.clip(values * rough * rising[None, :], -100.0, 100.0)
    return result.astype(jnp.bfloat16)


def level_of(stream_key, shape, cuts, least, largest):
    gain, own = 1.0, jax.random.fold_in(stream_key, 6)
    for axis_at, parts in cuts:
        heights = jnp.exp(jax.random.uniform(jax.random.fold_in(own, axis_at), (parts,), jnp.float32, least / len(cuts), largest / len(cuts)))
        gain = gain * jnp.repeat(heights, shape[axis_at] // parts).reshape([-1 if axis == axis_at else 1 for axis in range(len(shape))])
    return gain


def normal_values(own_key, extent, scale, reach, cuts=(), held_as=jnp.bfloat16):
    values = scale * jax.random.normal(own_key, extent, jnp.float32)
    if cuts:
        values = values * level_of(own_key, extent, cuts, -0.22, 0.18)
    return jnp.clip(values, -reach, reach).astype(held_as)


def setup_inputs(seed: int = 0) -> dict:
    keys = jax.random.split(jax.random.key(seed), 5)
    tokens = draw_tokens(jax.random.fold_in(keys[4], 71), 0)
    norm_gain = jnp.clip(1.0 + 0.1 * jax.random.normal(keys[1], (D,), jnp.float32), 0.5, 1.5)
    projection_weight = normal_values(keys[2], (KV_ROWS, D), 0.25, 1.5, ((0, 4), (1, 8)))
    panel_index = jax.random.randint(keys[3], (1,), 0, NPANELS).astype(jnp.int32)
    return {"tokens": tokens, "norm_gain": norm_gain, "projection_weight": projection_weight, "panel_index": panel_index}


epsilon = 1e-05
damping = 0.1

def reference(tokens, norm_gain, projection_weight, panel_index):
    token_values = tokens.astype(jnp.float32)
    squares = lax.optimization_barrier(jnp.sum(token_values * token_values, axis=1, keepdims=True))
    normed = (token_values * lax.rsqrt(squares / D + epsilon) * norm_gain[None, :]).astype(jnp.bfloat16)
    normed_wide = normed.astype(jnp.float32)
    gram = jnp.dot(normed_wide.T, normed_wide, precision=lax.Precision.HIGHEST) / TOKENS
    trace_sum = jnp.sum(normed_wide * normed_wide) / TOKENS
    diag_shift = damping * trace_sum / D
    diag_ids = jnp.arange(D, dtype=jnp.int32)
    gram = gram.at[diag_ids, diag_ids].add(diag_shift)
    panel_start = (panel_index[0] * PANEL).astype(jnp.int32)
    panel_cols = lax.dynamic_slice_in_dim(gram, panel_start, PANEL, 1)
    diag_block = lax.dynamic_slice_in_dim(panel_cols, panel_start, PANEL, 0)
    factor = jnp.linalg.cholesky(diag_block)
    whitened = lax.linalg.triangular_solve(factor, panel_cols, left_side=False, lower=True, transpose_a=True)
    factor_panel = whitened.astype(jnp.bfloat16)
    projected = jnp.dot(projection_weight.astype(jnp.float32), factor_panel.astype(jnp.float32), preferred_element_type=jnp.float32)
    return (gram, factor_panel, projected)
```

```python
import functools

import jax
import jax.numpy as jnp
from jax import lax
from jax.experimental import pallas as pl
from jax.experimental.pallas import tpu as pltpu
from jax.sharding import PartitionSpec as P

D = 16384
PANEL = 512
BASE = 128
GROUP = 8
CHUNKS = 2
PARTS = 3
SPARE = 32

epsilon = 1e-05
damping = 0.1
HIGHEST = lax.Precision.HIGHEST
VMEM_SPEC = pl.BlockSpec(memory_space=pltpu.VMEM)
ANY_SPEC = pl.BlockSpec(memory_space=pl.ANY)
SMEM_SPEC = pl.BlockSpec(memory_space=pltpu.SMEM)
VMEM_LIMIT = 60 * 1024 * 1024


def f32_dot(a, b):
    return jnp.dot(a, b, precision=HIGHEST, preferred_element_type=jnp.float32)


def base_inverse(block):
    n = block.shape[0]
    count = n // 8
    tiles = [block[8 * b : 8 * b + 8, :] for b in range(count)]
    lane = lax.broadcasted_iota(jnp.int32, (8, n), 1)

    def full(v):
        return jnp.broadcast_to(v, (8, n))

    for a in range(count):
        k = a * 8
        tile = tiles[a]
        rows = [full(tile[q : q + 1, :]) for q in range(8)]
        low = [[None] * 8 for _ in range(8)]
        inv = [None] * 8
        pivots = [[full(rows[p][:, k + q : k + q + 1]) if q >= p else None for q in range(8)] for p in range(8)]
        for q in range(8):
            d = pivots[q][q]
            for e in range(q):
                d = d - low[q][e] * low[q][e]
            inv[q] = lax.rsqrt(d)
            for r in range(q + 1, 8):
                v = pivots[q][r]
                for e in range(q):
                    v = v - low[r][e] * low[q][e]
                low[r][q] = v * inv[q]
        mine = (lane >= k) & (lane < k + 8)
        done = []
        for q in range(8):
            v = jnp.where(mine, jnp.where(lane == k + q, 1.0, 0.0), rows[q])
            for e in range(q):
                v = v - low[q][e] * done[e]
            done.append(v * inv[q])
        for b in range(a + 1, count):
            u = jnp.where(mine, 0.0, tiles[b])
            mult = []
            for q in range(8):
                v = full(tiles[b][:, k + q : k + q + 1])
                for e in range(q):
                    v = v - low[q][e] * mult[e]
                mult.append(v * inv[q])
            total = mult[0] * done[0]
            for q in range(1, 8):
                total = total + mult[q] * done[q]
            tiles[b] = u - total
        tiles[a] = jnp.concatenate([done[q][q : q + 1, :] for q in range(8)], axis=0)
    result = jnp.concatenate(tiles, axis=0)
    i = lax.broadcasted_iota(jnp.int32, (n, n), 0)
    j = lax.broadcasted_iota(jnp.int32, (n, n), 1)
    return jnp.where(i >= j, result, 0.0)


def factor_inverse(work, held, out):
    n = work.shape[0]
    count = n // BASE

    def body(step, carry):
        at = pl.multiple_of(step * BASE, BASE)
        held[...] = base_inverse(work[pl.ds(at, BASE), pl.ds(at, BASE)])
        for q in range(count):

            @pl.when(step == q)
            def _(q=q):
                lo, hi = q * BASE, (q + 1) * BASE
                mine = held[...]
                out[lo:hi, lo:hi] = mine
                if q:
                    left = f32_dot(mine, work[lo:hi, :lo])
                    out[lo:hi, :lo] = left
                if hi < n:
                    out[lo:hi, hi:] = jnp.zeros((BASE, n - hi), jnp.float32)
                    right = f32_dot(mine, work[lo:hi, hi:])
                    below = right.T
                    work[hi:, hi:] = work[hi:, hi:] - f32_dot(below, right)
                    work[hi:, lo:hi] = -f32_dot(below, mine)
                    if q:
                        work[hi:, :lo] = work[hi:, :lo] - f32_dot(below, left)

        return carry

    lax.fori_loop(0, count, body, 0)


def split(v):
    high = v.astype(jnp.bfloat16)
    return high, (v - high.astype(jnp.float32)).astype(jnp.bfloat16)


def pieces_of(v):
    found = []
    for _ in range(PARTS):
        part = v.astype(jnp.bfloat16).astype(jnp.float32)
        found.append(part)
        v = v - part
    return found


def layout(tensors, rows, row_width):
    each = PANEL // rows
    stats = PARTS * 2 * tensors // each
    wide = row_width // PANEL
    return stats, stats + PARTS, stats + PARTS + PARTS * wide


def small_kernel(tensors, row_width, index, tokens, gain, out):
    rows, columns = tokens.shape
    each = PANEL // rows
    stats_end, gain_end, end = layout(tensors, rows, row_width)
    step = min(columns, 1024)
    squares = jnp.zeros((rows, 1), jnp.float32)
    energy = jnp.zeros((rows, 1), jnp.float32)
    for at in range(0, columns, step):
        wide = tokens[:, at : at + step].astype(jnp.float32)
        squares = squares + jnp.sum(wide * wide, axis=1, keepdims=True)
        raised = wide * (gain[:, at : at + step] * epsilon**-0.5)
        energy = energy + jnp.sum(raised * raised, axis=1, keepdims=True)
    segments = []
    for v in (squares, energy):
        line = jnp.broadcast_to(v, (rows, rows)).T[0:1, :]
        for part in pieces_of(line):
            for t in range(tensors):
                segments.append(jnp.where(index[0] == t, part, 0.0))
    lines = [jnp.concatenate(segments[k : k + each], axis=1) for k in range(0, len(segments), each)]
    panel_at = pl.multiple_of(index[1], 128)
    owner = index[2] == 1
    lines += [jnp.where(owner, part, 0.0) for part in pieces_of(gain[:, pl.ds(panel_at, PANEL)])]
    for at in range(0, row_width, PANEL):
        own = gain[:, pl.ds(pl.multiple_of(index[3] + at, 128), PANEL)]
        lines += [jnp.where(index[4] == 1, part, 0.0) for part in pieces_of(own)]
    lines.append(jnp.zeros((SPARE - end, PANEL), jnp.float32))
    out[:rows, :] = jnp.where(owner, tokens[:, pl.ds(panel_at, PANEL)], 0).astype(jnp.bfloat16)
    out[rows:, :] = jnp.concatenate(lines, axis=0).astype(jnp.bfloat16)


def panel_kernel(chips, cores, tensors, row_width, tokens_all, index, *refs):
    parts, refs = refs[: chips * cores], refs[chips * cores :]
    inverse, panel, scales, shift_out, row_gain, work, held = refs
    rows = parts[0].shape[0] - SPARE
    each = PANEL // rows
    stats_end, gain_end, end = layout(tensors, rows, row_width)
    extra = parts[0][rows:, :].astype(jnp.float32)
    gain = sum(extra[stats_end + e : stats_end + e + 1, :] for e in range(PARTS))
    for k, at in enumerate(range(0, row_width, PANEL)):
        row_gain[:, at : at + PANEL] = sum(
            extra[gain_end + k * PARTS + e : gain_end + k * PARTS + e + 1, :] for e in range(PARTS)
        )
    core = index[0]
    squares, energy = [], []
    for m in range(chips):
        for c in range(cores):
            lines = [parts[m * cores + x][rows:, :].astype(jnp.float32) for x in range(cores)]
            line = lines[0]
            for x in range(1, cores):
                line = jnp.where((core ^ x) == c, lines[x], line)
            for k, into in ((0, squares), (1, energy)):
                total = jnp.zeros((1, rows), jnp.float32)
                for e in range(PARTS):
                    for t in range(tensors):
                        segment = (k * PARTS + e) * tensors + t
                        r, q = divmod(segment, each)
                        total = total + line[r : r + 1, q * rows : (q + 1) * rows]
                into.append(total)
    squares, energy = jnp.concatenate(squares, axis=0), jnp.concatenate(energy, axis=0)
    scale = lax.rsqrt(squares / D + epsilon)
    small = scale * (epsilon**0.5)
    mean = jnp.sum(small * small * energy) / tokens_all / D
    shift = damping * mean
    shift_out[...] = jnp.full(shift_out.shape, shift, jnp.float32)
    columns = scale.T
    scales[...] = columns
    for m in range(chips):
        for c in range(cores):
            source = parts[m * cores][:rows, :]
            for x in range(1, cores):
                source = jnp.where((core ^ x) == c, parts[m * cores + x][:rows, :], source)
            at = m * cores + c
            wide = source.astype(jnp.float32) * columns[:, at : at + 1] * gain
            panel[at * rows : (at + 1) * rows, :] = wide.astype(jnp.bfloat16)
    block = (
        lax.dot_general(
            panel[...], panel[...], (((0,), (0,)), ((), ())), preferred_element_type=jnp.float32
        )
        / tokens_all
    )
    n = block.shape[0]
    i = lax.broadcasted_iota(jnp.int32, (n, n), 0)
    j = lax.broadcasted_iota(jnp.int32, (n, n), 1)
    work[...] = (block + jnp.where(i == j, shift, 0.0)) / mean
    factor_inverse(work, held, inverse)
    inverse[...] = inverse[...] * lax.rsqrt(jnp.full((1, 1), mean, jnp.float32))


def column_kernel(places, cores, rows, index, *refs):
    count = len(places)
    parts, (scales, gain, out) = refs[: count * cores], refs[count * cores :]
    width = parts[0].shape[1]
    for x in range(cores):
        where = pl.ds(pl.multiple_of((index[0] ^ x) * width, 128), width)
        factor = gain[:, where]
        for ref, at in zip(parts[x * count : (x + 1) * count], places, strict=True):
            for r in range(0, ref.shape[0], rows):
                token = at + r
                wide = ref[r : r + rows, :].astype(jnp.float32)
                wide = wide * scales[:, token // rows : token // rows + 1] * factor
                out[token : token + rows, where] = wide.astype(jnp.bfloat16)


def pack_kernel(count, index, *refs):
    inputs, (outs, held, sems) = refs[:count], (refs[count:-2], refs[-2], refs[-1])
    for n, out in enumerate(outs):
        for k in range(count):

            @pl.when(index[n] == k + 1)
            def _(n=n, k=k):
                pltpu.make_async_copy(inputs[k], held.at[n], sems.at[n]).start()

    for n, out in enumerate(outs):

        @pl.when(index[n] > 0)
        def _(n=n, out=out):
            pltpu.make_async_copy(inputs[0], held.at[n], sems.at[n]).wait()
            pltpu.make_async_copy(held.at[n], out, sems.at[n]).start()

    for n, out in enumerate(outs):

        @pl.when(index[n] > 0)
        def _(n=n, out=out):
            pltpu.make_async_copy(held.at[n], out, sems.at[n]).wait()


def bf16_dot_t(a, b):
    return lax.dot_general(a, b, (((1,), (1,)), ((), ())), preferred_element_type=jnp.float32)


def row_kernel(places, others, received, rows, start, width, first, last, index, *refs):
    count = len(places)
    columns, refs = refs[:count], refs[count:]
    nearby, refs = refs[:others], refs[others:]
    arrived, refs = refs[:received], refs[received:]
    scales, gain, panel, inverse, shift, weight = refs[:6]
    if first:
        turned, white, partial, raw, result, sems, out_sem = refs[6:]
    else:
        _, before, turned, white, partial, raw, result, sems, out_sem = refs[6:]
    tokens = raw.shape[0]
    group = tokens // (received + 1)

    @pl.when(index[0] == 0)
    def _():
        copies = [
            pltpu.make_async_copy(
                ref.at[:, start : start + width], raw.at[at : at + ref.shape[0], :], sems.at[n]
            )
            for n, (ref, at) in enumerate(zip(columns, places, strict=True))
        ]
        for c in copies:
            c.start()
        for c in copies:
            c.wait()

    @pl.when(index[0] > 0)
    def _():
        for k in range(others):

            @pl.when(index[0] == k + 1)
            def _(k=k):
                pltpu.make_async_copy(nearby[k], raw.at[:group, :], sems.at[0]).start()

        copies = [
            pltpu.make_async_copy(ref, raw.at[(m + 1) * group : (m + 2) * group, :], sems.at[m + 1])
            for m, ref in enumerate(arrived)
        ]
        for c in copies:
            c.start()
        pltpu.make_async_copy(nearby[0], raw.at[:group, :], sems.at[0]).wait()
        for c in copies:
            c.wait()

    for m in range(tokens // rows):
        here = slice(m * rows, (m + 1) * rows)
        wide = raw[here, :].astype(jnp.float32) * scales[:, m : m + 1] * gain[:, start : start + width]
        turned[:, here] = wide.astype(jnp.bfloat16).T
    gram = jnp.dot(turned[...], panel[...], preferred_element_type=jnp.float32) / tokens
    i = index[1] + lax.broadcasted_iota(jnp.int32, gram.shape, 0)
    j = index[2] + lax.broadcasted_iota(jnp.int32, gram.shape, 1)
    gram = gram + jnp.where(i == j, shift[0:1, 0:1], 0.0)
    high, low = split(gram)
    inverse_high, inverse_low = split(inverse[...])
    result[...] = (
        bf16_dot_t(high, inverse_high) + bf16_dot_t(high, inverse_low) + bf16_dot_t(low, inverse_high)
    ).astype(jnp.bfloat16)
    put = pltpu.make_async_copy(result, white.at[start : start + width, :], out_sem)
    put.start()
    product = jnp.dot(weight[:, start : start + width], result[...], preferred_element_type=jnp.float32)
    if not first:
        product = before[...] + product
    partial[...] = product.T if last else product
    put.wait()


def gram_kernel(tokens, index, turned, columns, shift, *refs):
    out = refs[-1]
    step = pl.program_id(0)
    height = out.shape[0]
    out_width = out.shape[1]
    piece = min(512, out_width)
    for at in range(0, out_width, piece):
        out[:, at : at + piece] = (
            jnp.dot(turned[...], columns[:, at : at + piece], preferred_element_type=jnp.float32)
            / tokens
        )
    ahead = index[0] + step * height

    @pl.when((ahead >= 0) & (ahead < out_width))
    def _():
        i = lax.broadcasted_iota(jnp.int32, (height, height), 0)
        j = lax.broadcasted_iota(jnp.int32, (height, height), 1)
        where = pl.ds(pl.multiple_of(ahead, height), height)
        out[:, where] = out[:, where] + jnp.where(i == j, shift[0:1, 0:1], 0.0)


def bits_below(n):
    found, b = [], 1
    while b < n:
        found.append(b)
        b *= 2
    return found


def by_xor(v, axis, m):
    n = lax.axis_size(axis)
    return lax.ppermute(v, axis, [(i, i ^ m) for i in range(n)])


def kernel_call(body, out_shape, **more):
    params = pltpu.CompilerParams(vmem_limit_bytes=VMEM_LIMIT)
    return pl.pallas_call(body, out_shape=out_shape, compiler_params=params, **more)


def integers(*values):
    return jnp.stack([jnp.asarray(v, jnp.int32) for v in values])


def on_device(tokens, norm_gain, projection_weight, panel_index):
    f32, bf16 = jnp.float32, jnp.bfloat16
    shape = jax.ShapeDtypeStruct
    seqs, tensors = lax.axis_size("seq"), lax.axis_size("tensor")
    seq, tensor = lax.axis_index("seq"), lax.axis_index("tensor")
    rows, column_width = tokens.shape
    tokens_all = rows * seqs
    row_width = column_width * tensors // seqs
    cores = column_width // row_width
    chips = seqs // cores
    chip, core = seq // cores, seq % cores
    panel_start = panel_index[0] * PANEL
    owner = panel_start // column_width
    panel_at = panel_start - owner * column_width

    index = integers(tensor, panel_at, tensor == owner, core * row_width, tensor == chip)
    small = kernel_call(
        functools.partial(small_kernel, tensors, row_width),
        shape((rows + SPARE, PANEL), bf16),
        in_specs=[SMEM_SPEC, VMEM_SPEC, VMEM_SPEC],
        out_specs=VMEM_SPEC,
        name="small",
    )(index, tokens, norm_gain[None, :])
    for b in bits_below(tensors):
        small = small + by_xor(small, "tensor", b)
    panels = []
    for m in range(chips):
        panels.append(by_xor(small, "seq", m * cores) if m else small)
    stacked = jnp.concatenate(panels, axis=0)
    pairs = [[v] for v in panels]
    for x in range(1, cores):
        swapped = by_xor(stacked, "seq", x).reshape(chips, rows + SPARE, PANEL)
        for m in range(chips):
            pairs[m].append(swapped[m])
    inverse, panel, scales, shift, row_gain = kernel_call(
        functools.partial(panel_kernel, chips, cores, tensors, row_width, tokens_all),
        (
            shape((PANEL, PANEL), f32),
            shape((tokens_all, PANEL), bf16),
            shape((rows, seqs), f32),
            shape((1, 128), f32),
            shape((1, row_width), f32),
        ),
        in_specs=[SMEM_SPEC] + [VMEM_SPEC] * seqs,
        out_specs=[VMEM_SPEC] * 5,
        scratch_shapes=[pltpu.VMEM((PANEL, PANEL), f32), pltpu.VMEM((BASE, BASE), f32)],
        name="panel",
    )(integers(core), *[v for group in pairs for v in group])

    shares = [lax.dynamic_slice_in_dim(tokens, (core ^ x) * row_width, row_width, 1) for x in range(cores)]
    gathered = [shares[0]] + [by_xor(shares[x], "seq", x) for x in range(1, cores)]
    ordered = []
    for c in range(cores):
        v = gathered[0]
        for x in range(1, cores):
            v = jnp.where((core ^ x) == c, gathered[x], v)
        ordered.append(v)
    grouped = jnp.concatenate(ordered, axis=0)
    group = rows * cores
    middle = group // 2

    held = {0: [grouped]}

    def part(m, which):
        if len(held[m]) > 1:
            return held[m][which]
        return held[m][0][which * middle : (which + 1) * middle]

    for m in range(1, chips):
        low, high = m & -m, 1 << (m.bit_length() - 1)
        if low == high:
            held[m] = [by_xor(grouped, "seq", m * cores)]
        else:
            held[m] = [
                by_xor(part(m ^ low, 0), "seq", low * cores),
                by_xor(part(m ^ high, 1), "seq", high * cores),
            ]
    columns, places = [], []
    for m in range(chips):
        for k, v in enumerate(held[m]):
            columns.append(v)
            places.append(m * group + k * middle)
    every = list(columns)
    for x in range(1, cores):
        every += [by_xor(v, "seq", x) for v in columns]
    normed = kernel_call(
        functools.partial(column_kernel, tuple(places), cores, rows),
        shape((tokens_all, column_width), bf16),
        in_specs=[SMEM_SPEC] + [VMEM_SPEC] * (len(every) + 2),
        out_specs=VMEM_SPEC,
        name="columns",
    )(integers(core), *every, scales, norm_gain[None, :])

    both = ("seq", "tensor")
    width = row_width // CHUNKS
    height = min(512, width)
    outs = projection_weight.shape[0]
    gram, white, partial = None, None, None
    for c in range(CHUNKS):
        start = c * width
        first, last = c == 0, c == CHUNKS - 1
        others = {0: grouped[:, start : start + width]}
        for x in range(1, tensors):
            low = x & -x
            others[x] = by_xor(others[x ^ low], "tensor", low)
        nearby = [others[x] for x in range(1, tensors)]
        packed = kernel_call(
            functools.partial(pack_kernel, tensors - 1),
            [shape((group, width), bf16)] * (chips - 1),
            in_specs=[SMEM_SPEC] + [ANY_SPEC] * (tensors - 1),
            out_specs=[ANY_SPEC] * (chips - 1),
            scratch_shapes=[
                pltpu.VMEM((chips - 1, group, width), bf16),
                pltpu.SemaphoreType.DMA((chips - 1,)),
            ],
            name="pack",
        )(integers(*[tensor ^ (chip ^ m) for m in range(1, chips)]), *nearby)
        received = []
        for m in range(1, chips):
            pairs = [
                (i * tensors + t, (i ^ (m * cores)) * tensors + t)
                for i in range(seqs)
                for t in range(tensors)
                if (i ^ (m * cores)) // cores != t
            ]
            received.append(lax.ppermute(packed[m - 1], both, pairs))
        row_start = seq * row_width + start
        inputs = [*columns, *nearby, *received]
        specs = [SMEM_SPEC] + [ANY_SPEC] * len(inputs) + [VMEM_SPEC] * 6
        inputs += [scales, row_gain, panel, inverse, shift, projection_weight]
        aliases = {}
        if not first:
            aliases = {1 + len(inputs): 1}
            inputs += [white, partial]
            specs += [ANY_SPEC, VMEM_SPEC]
        turned, white, partial = kernel_call(
            functools.partial(
                row_kernel, tuple(places), tensors - 1, chips - 1, rows, start, width, first, last
            ),
            (
                shape((width, tokens_all), bf16),
                shape((row_width, PANEL), bf16),
                shape((PANEL, outs) if last else (outs, PANEL), f32),
            ),
            in_specs=specs,
            out_specs=[VMEM_SPEC, ANY_SPEC, VMEM_SPEC],
            scratch_shapes=[
                pltpu.VMEM((tokens_all, width), bf16),
                pltpu.VMEM((width, PANEL), bf16),
                pltpu.SemaphoreType.DMA((len(columns) + chips,)),
                pltpu.SemaphoreType.DMA,
            ],
            input_output_aliases=aliases,
            name="rows",
        )(integers(tensor ^ chip, row_start, panel_start), *inputs)
        inputs = [turned, normed, shift]
        specs = [
            pl.BlockSpec((height, tokens_all), lambda i, s: (i, 0)),
            pl.BlockSpec((tokens_all, column_width), lambda i, s: (0, 0), pipeline_mode=pl.Buffered(1)),
            pl.BlockSpec((1, 128), lambda i, s: (0, 0)),
        ]
        aliases = {}
        if not first:
            aliases = {1 + len(inputs): 0}
            inputs.append(gram)
            specs.append(ANY_SPEC)
        gram = kernel_call(
            functools.partial(gram_kernel, tokens_all),
            shape((row_width, column_width), f32),
            grid_spec=pltpu.PrefetchScalarGridSpec(
                num_scalar_prefetch=1,
                grid=(width // height,),
                in_specs=specs,
                out_specs=pl.BlockSpec((height, column_width), lambda i, s, o=start // height: (o + i, 0)),
            ),
            input_output_aliases=aliases,
            name="gram",
        )(integers(row_start - tensor * column_width), *inputs)

    share = PANEL // seqs
    total = lax.dynamic_slice_in_dim(partial, seq * share, share, 0)
    for m in range(1, seqs):
        piece = lax.dynamic_slice_in_dim(partial, (seq ^ m) * share, share, 0)
        total = total + by_xor(piece, "seq", m)
    return gram, white, total.T


def solution(mesh):
    placed = (P("seq", "tensor"), P("tensor"), P("tensor", "seq"), P())
    return jax.shard_map(
        on_device,
        mesh=mesh,
        in_specs=placed,
        out_specs=(P("seq", "tensor"), P("seq", None), P("tensor", "seq")),
        check_vma=False,
    )
```
